32 devices in a mesh: ens: 2 (over x), lon: 16 (over z, y, core).
Axes of the slice: x: 2, y: 2, z: 4, core: 2. Of those that a mesh axis runs over, the one named last changes fastest.
Arguments:
- tracer: float32 [4, 256, 75, 256], P(None, 'lon', None, 'ens'), parts along dimension 3, may hold values from -6 to 6
- east_speed: float32 [256, 75, 256], P('lon', None, 'ens'), parts along dimension 2, may hold values from -0.25 to 0.25
- north_speed: float32 [256, 75, 256], P('lon', None, 'ens'), parts along dimension 2, may hold values from -0.25 to 0.25
- diffusivity: float32 [256, 75, 256], P('lon', None, 'ens'), parts along dimension 2, may hold values from 0.02 to 0.2
- mixing: float32 [256, 75, 256], P('lon', None, 'ens'), parts along dimension 2, may hold values from 0.05 to 5
- thickness: float32 [256, 75, 256], P('lon', None, 'ens'), parts along dimension 2, may hold values from 0.5 to 2
- depth_levels: int32 [256, 256], P('lon', 'ens'), parts along dimension 1, may hold values from 0 to 75
- air_flux: float32 [8, 4096], P('ens', 'lon'), parts along dimension 0, may hold values from -6 to 6
- margin_tile: int32 [32768, 1], P(('ens', 'lon')), parts along dimension 0, may hold values from 0 to 15; in each aligned block of 1024 rows (0 to 1023, 1024 to 2047, ...) at most 64 rows name the same one
- margin_source: int32 [32768], P(('ens', 'lon')), parts along dimension 0, may hold values from 0 to 255
- margin_cell: int32 [32768], P(('ens', 'lon')), parts along dimension 0, may hold values from 0 to 2047
- margin_weight: float32 [32768], P(('ens', 'lon')), parts along dimension 0, may hold values from 0.2 to 1
Outputs:
- tracer_next: float32 [4, 256, 75, 256], P(None, 'lon', None, 'ens'), parts along dimension 3
The draws below stay inside these ranges and needn't reach their ends.
There are 2 independent parts, one for each index of `ens`. The reference program is written for one: setup_inputs(seed, part) draws one part's arguments, and reference() takes and returns one part's arrays. A program takes and returns all parts, laid end to end along the dimension named above; each array names one. Nothing has to cross between parts.
Inputs may be any that keep to these rules, and one draw needn't show every extreme that they name: `margin_tile`: the rows of one tile name each ocean tile at most 64 times.
All inputs are finite; a program needn't handle non-finite values.
Results may differ from the reference program's by a relative error of at most 0.00002.
Values sent between devices are 32-bit elements; how exact they have to be, the bound alone decides.
A program may use at most 192 MiB of HBM per device.

```python
import math
import jax
import jax.numpy as jnp
import numpy as np

LX = 16
NY = 128
NZ = 75
TRACERS = 4
ACELL_DEV = 256
OVL_DEV = 1024
CAP = 64
NX = 256
ACELLS = 4096
OVL = 16384
N_LON = 16


def touch_ends(entries, own_key, least, top_value):
    shape = entries.shape
    place = [jax.random.randint(jax.random.fold_in(own_key, axis), (), 0, shape[axis]) for axis in range(len(shape))]
    entries = entries.at[tuple(place)].set(least)
    longest = shape.index(max(shape))
    place[longest] = (place[longest] + 1) % shape[longest]
    return entries.at[tuple(place)].set(top_value)


def block_scale(key, extent, cuts, least, high):
    loudness, own = 1.0, jax.random.fold_in(key, 6)
    for position, parts in cuts:
        draws = jnp.exp(jax.random.uniform(jax.random.fold_in(own, position), (parts,), jnp.float32, least / len(cuts), high / len(cuts)))
        loudness = loudness * jnp.repeat(draws, extent[position] // parts).reshape([-1 if axis == position else 1 for axis in range(len(extent))])
    return loudness


def shared_out(key, own, number, rows, amount, top, bound, lean):
    ranking = jax.random.permutation(key, amount)
    heavy_load, ordinary = portions_of(amount, rows * top, bound, lean, True), portions_of(amount, rows * top, bound, lean, False)
    places = jnp.arange(amount)

    def named(lengths, rotation):
        used = int((lengths > 0).sum())
        fixed = max(1, used // 4)
        shifted = fixed + (places - fixed + rotation * (used - fixed)) % max(1, amount - fixed)
        return jnp.zeros((amount,), jnp.int32).at[ranking[jnp.where(places < fixed, places, shifted)]].set(jnp.asarray(lengths, jnp.int32))

    lengths = jnp.where(number % 4 == 0, named(heavy_load, number // 4), named(ordinary, number - number // 4 - 1))
    mixed = jax.random.permutation(jax.random.fold_in(own, 3), amount)
    giver, sink = mixed[0:amount // 2 * 2:2], mixed[1:amount // 2 * 2:2]
    margin = jnp.minimum(lengths[giver] - 1, bound - lengths[sink]) // 2
    margin = jnp.where((giver == ranking[0]) | (sink == ranking[0]) | (lengths[sink] == 0), 0, jnp.maximum(margin, 0))
    shifted = jax.random.randint(jax.random.fold_in(own, 4), (amount // 2,), 0, 1 << 20) % (margin + 1)
    lengths = lengths.at[giver].add(-shifted).at[sink].add(shifted)
    items = jnp.searchsorted(jnp.cumsum(lengths), jnp.arange(rows * top), side="right").astype(jnp.int32)
    listing = items.reshape(top, rows).T
    listing = listing[jax.random.permutation(jax.random.fold_in(own, 1), rows)]
    rotation = jax.random.randint(jax.random.fold_in(own, 2), (rows, 1), 0, top)
    return jnp.take_along_axis(listing, (jnp.arange(top)[None, :] + rotation) % top, axis=1)


def portions_of(number_of, total, most, slope, full):
    loads = [(1 << 20) // math.isqrt(rank ** slope) + 1 for rank in range(1, number_of + 1)]
    largest = most if full else min(most, max(-(-total // number_of), total * loads[0] // sum(loads)))
    least = 1 if total - largest >= number_of - 1 else 0
    given, surplus = [largest] + [least] * (number_of - 1), total - largest - least * (number_of - 1)
    while surplus > 0:
        candidates = [i for i in range(1, number_of) if given[i] < largest] or [i for i in range(1, number_of) if given[i] < most]
        pool, left = sum([loads[i] for i in candidates]), surplus
        for i in candidates:
            extra = min(most - given[i], max(1, left * loads[i] // pool), surplus)
            given[i] = given[i] + extra
            surplus = surplus - extra
    return np.array(given)


def bell_draw(own_key, dims, deviation, most, pieces=(), kind=jnp.bfloat16):
    result = deviation * jax.random.normal(own_key, dims, jnp.float32)
    if pieces:
        result = result * block_scale(own_key, dims, pieces, -0.22, 0.18)
    return jnp.clip(result, -most, most).astype(kind)


def setup_inputs(seed: int = 0, part: int = 0) -> dict:
    keys = jax.random.split(jax.random.key(seed), 13)
    own_keys = jax.random.split(jax.random.fold_in(keys[12], part), 13)
    tracer = bell_draw(own_keys[0], (TRACERS, NX, NZ, NY), 1.0, 6.0, ((1, 16),), jnp.float32)
    east_speed = jnp.clip(jax.random.uniform(own_keys[1], (NX, NZ, NY), jnp.float32, -0.25, 0.25) * block_scale(own_keys[1], (NX, NZ, NY), ((0, 16),), -0.4, 0.0), -0.25, 0.25)
    north_speed = jnp.clip(jax.random.uniform(own_keys[2], (NX, NZ, NY), jnp.float32, -0.25, 0.25) * block_scale(own_keys[2], (NX, NZ, NY), ((0, 16),), -0.4, 0.0), -0.25, 0.25)
    diffusivity = jnp.clip(jnp.exp(math.log(0.2) - 2.3025851 * jax.random.uniform(own_keys[3], (NX, NZ, NY), jnp.float32) ** block_scale(own_keys[3], (NX, NZ, NY), ((0, 16),), -0.2, 0.2)), 0.02, 0.2)
    mixing = jnp.clip(jnp.exp(math.log(5.0) - 4.6051702 * jax.random.uniform(own_keys[4], (NX, NZ, NY), jnp.float32) ** block_scale(own_keys[4], (NX, NZ, NY), ((0, 16),), -0.2, 0.2)), 0.05, 5.0)
    thickness = jnp.clip(jnp.exp(math.log(2.0) - 1.3862944 * jax.random.uniform(own_keys[5], (NX, NZ, NY), jnp.float32) ** block_scale(own_keys[5], (NX, NZ, NY), ((0, 16),), -0.2, 0.2)), 0.5, 2.0)
    depth_levels = touch_ends(jax.random.randint(own_keys[6], (NX, NY), 0, NZ + 1), jax.random.fold_in(own_keys[6], 1), 0, NZ).astype(jnp.int32)
    air_flux = bell_draw(own_keys[7], (TRACERS, ACELLS), 1.0, 6.0, ((1, 16),), jnp.float32)
    margin_tile_keys = jax.random.split(jax.random.fold_in(own_keys[8], 1), OVL // OVL_DEV)
    margin_tile_turns = jax.random.permutation(jax.random.fold_in(own_keys[8], 3), OVL // OVL_DEV)
    margin_tile = jax.vmap(lambda own, number: shared_out(jax.random.fold_in(own_keys[8], 2), own, number, OVL_DEV, N_LON, 1, CAP, 2))(margin_tile_keys, margin_tile_turns).reshape((OVL, 1))
    margin_source = touch_ends(jax.random.randint(own_keys[9], (OVL,), 0, ACELL_DEV), jax.random.fold_in(own_keys[9], 1), 0, ACELL_DEV - 1).astype(jnp.int32)
    margin_cell = touch_ends(jax.random.randint(own_keys[10], (OVL,), 0, LX * NY), jax.random.fold_in(own_keys[10], 1), 0, (LX * NY) - 1).astype(jnp.int32)
    margin_weight = jnp.clip(0.2 + 0.8 * jax.random.uniform(own_keys[11], (OVL,), jnp.float32) ** block_scale(own_keys[11], (OVL,), ((0, 16),), -0.2, 0.2), 0.2, 1.0)
    return {"tracer": tracer, "east_speed": east_speed, "north_speed": north_speed, "diffusivity": diffusivity, "mixing": mixing, "thickness": thickness, "depth_levels": depth_levels, "air_flux": air_flux, "margin_tile": margin_tile, "margin_source": margin_source, "margin_cell": margin_cell, "margin_weight": margin_weight}


def face_flux(speed, kappa_near, kappa_far, open_face, near, far):
    return open_face * (jnp.maximum(speed, 0.0) * near + jnp.minimum(speed, 0.0) * far + 0.5 * (kappa_near + kappa_far) * (near - far))


def mix_columns(stepped, mixing, thickness, wet_mask, surface):
    levels = stepped.shape[2]
    wet_below = jnp.concatenate([wet_mask[:, 1:], jnp.zeros_like(wet_mask[:, :1])], axis=1)
    thickness_below = jnp.concatenate([thickness[:, 1:], thickness[:, -1:]], axis=1)
    coupling = mixing * wet_below / (0.5 * (thickness + thickness_below))
    prior_coupling = jnp.zeros_like(thickness[:, 0])
    prior_gain = jnp.zeros_like(thickness[:, 0])
    prior_value = jnp.zeros_like(stepped[:, :, 0])
    gain_list = []
    value_list = []
    for level_index in range(levels):
        here_coupling = coupling[:, level_index]
        here_thickness = thickness[:, level_index]
        pivot_value = here_thickness + here_coupling + prior_coupling - prior_coupling * prior_gain
        right_side = here_thickness * stepped[:, :, level_index]
        if level_index == 0:
            right_side = right_side + wet_mask[:, 0] * surface
        prior_value = (right_side + prior_coupling * prior_value) / pivot_value
        prior_gain = here_coupling / pivot_value
        prior_coupling = here_coupling
        gain_list.append(prior_gain)
        value_list.append(prior_value)
    solved = [value_list[-1]]
    for level_index in range(levels - 2, -1, -1):
        solved.append(value_list[level_index] + gain_list[level_index] * solved[-1])
    return jnp.stack(solved[::-1], axis=2)


def reference(tracer, east_speed, north_speed, diffusivity, mixing, thickness, depth_levels, air_flux, margin_tile, margin_source, margin_cell, margin_weight):
    level_ids = jnp.arange(NZ).astype(jnp.int32)
    wet_mask = (level_ids[None, :, None] < depth_levels[:, None, :]).astype(jnp.float32)
    east_flux = face_flux(east_speed[None], diffusivity[None], jnp.roll(diffusivity, -1, axis=0)[None], (wet_mask * jnp.roll(wet_mask, -1, axis=0))[None], tracer, jnp.roll(tracer, -1, axis=1))
    zonal_change = east_flux - jnp.roll(east_flux, 1, axis=1)
    mirror_tracer = jnp.flip(tracer[:, :, :, -1], axis=1)
    mirror_speed = jnp.flip(north_speed[:, :, -1], axis=0)
    mirror_kappa = jnp.flip(diffusivity[:, :, -1], axis=0)
    mirror_wet = jnp.flip(wet_mask[:, :, -1], axis=0)
    fold_flux = face_flux((0.5 * (north_speed[:, :, -1] - mirror_speed))[None], diffusivity[None, :, :, -1], mirror_kappa[None], (wet_mask[:, :, -1] * mirror_wet)[None], tracer[:, :, :, -1], mirror_tracer)
    inner_flux = face_flux(north_speed[None, :, :, :-1], diffusivity[None, :, :, :-1], diffusivity[None, :, :, 1:], (wet_mask[:, :, :-1] * wet_mask[:, :, 1:])[None], tracer[:, :, :, :-1], tracer[:, :, :, 1:])
    north_flux = jnp.concatenate([inner_flux, fold_flux[..., None]], axis=3)
    south_flux = jnp.concatenate([jnp.zeros_like(inner_flux[..., :1]), inner_flux], axis=3)
    stepped = tracer - zonal_change - (north_flux - south_flux)
    owner = (jnp.arange(OVL) // OVL_DEV).astype(jnp.int32)
    source = owner * ACELL_DEV + margin_source
    payload = margin_weight[None, :] * jnp.take(air_flux, source, axis=1)
    target = margin_tile[:, 0] * (LX * NY) + margin_cell
    surface = jnp.zeros((TRACERS, NX * NY), jnp.float32).at[:, target].add(payload).reshape(TRACERS, NX, NY)
    return mix_columns(stepped, mixing, thickness, wet_mask, surface)
```

```python
import jax
import jax.numpy as jnp
from jax import lax
from jax.experimental import pallas as pl
from jax.experimental.pallas import tpu as pltpu
from jax.sharding import PartitionSpec as P

CAP = 64
LANES = 128
ROWS = 16
F32 = jnp.float32
BF16 = jnp.bfloat16
I32 = jnp.int32


def iota(shape, axis):
    return lax.broadcasted_iota(I32, shape, axis)


def thirds(x):
    high = x.astype(BF16).astype(F32)
    rest = x - high
    middle = rest.astype(BF16).astype(F32)
    return high, middle, rest - middle


def prepare(tiles, tile_ref, source_ref, cell_ref, weight_ref, air_ref, tracer_ref, north_ref,
            kappa_ref, top_ref, send_ref):
    count, lon_cells = tracer_ref.shape[:2]
    records = tile_ref.shape[1]
    air_cells = air_ref.shape[1]
    lane = iota((tracer_ref.shape[2], LANES), 1)

    def take(i, packed):
        columns = [tracer_ref[n, i] for n in range(count)] + [north_ref[i], kappa_ref[i]]
        for f, column in enumerate(columns):
            spot = f * lon_cells + i
            packed = jnp.where(lane == spot, pltpu.roll(column, spot + 1, 1), packed)
        return packed

    top_ref[...] = lax.fori_loop(0, lon_cells, take, jnp.zeros(top_ref.shape, F32))

    picks = (iota((air_cells, records), 0) == source_ref[...]).astype(F32).astype(BF16)
    parts = jnp.concatenate(thirds(air_ref[...]), axis=0).astype(BF16)
    found = jnp.dot(parts, picks, preferred_element_type=F32)
    found = found[:count] + (found[count:2 * count] + found[2 * count:])
    payload = weight_ref[...] * found

    chosen = (iota((tiles, records), 0) == tile_ref[...]).astype(F32)
    earlier = (iota((LANES, LANES), 0) < iota((LANES, LANES), 1)).astype(F32).astype(BF16)
    carried = jnp.zeros((tiles, 1), F32)
    slots = []
    for start in range(0, records, LANES):
        piece = chosen[:, start:start + LANES]
        rank = jnp.dot(piece.astype(BF16), earlier, preferred_element_type=F32) + carried
        slots.append(jnp.sum(piece * rank, axis=0, keepdims=True))
        carried = carried + jnp.sum(piece, axis=1, keepdims=True)
    slot = jnp.concatenate(slots, axis=1)
    places = (iota((CAP, records), 0).astype(F32) == slot).astype(F32).astype(BF16)

    cells = cell_ref[...]
    row = (cells // LANES).astype(F32)
    column = (cells % LANES).astype(F32)
    lines = [p[n:n + 1] for p in thirds(payload) for n in range(count)] + [row, column]
    spread = jnp.concatenate([(chosen * line).astype(BF16) for line in lines], axis=0)
    packed = lax.dot_general(spread, places, (((1,), (1,)), ((), ())), preferred_element_type=F32)

    def part(index):
        return packed[index * tiles:(index + 1) * tiles]

    send_ref[...] = jnp.zeros(send_ref.shape, F32)
    for n in range(count):
        send_ref[:, n, :CAP] = part(n) + (part(count + n) + part(2 * count + n))
    send_ref[:, count, :CAP] = part(3 * count)
    send_ref[:, count + 1, :CAP] = part(3 * count + 1)


def exchange(tiles, tracer, east, kappa, depth, top, send,
             west_tracer, west_speed, west_kappa, west_depth, east_tracer, east_kappa, east_depth,
             mirror, mirror_depth, received, out_sems, in_sems, pair_out, pair_in, own_sem):
    me = lax.axis_index("lon")
    right = lax.rem(me + 1, tiles)
    left = lax.rem(me + tiles - 1, tiles)
    partner = tiles - 1 - me
    last = tracer.shape[1] - 1
    barrier = pltpu.get_barrier_semaphore()

    @pl.loop(1, tiles)
    def _(step):
        pl.semaphore_signal(barrier, inc=1, device_id={"lon": lax.rem(me + step, tiles)},
                            device_id_type=pl.DeviceIdType.MESH)

    pl.semaphore_wait(barrier, tiles - 1)
    plan = [
        (top, mirror, partner),
        (depth, mirror_depth, partner),
        (tracer.at[:, last], west_tracer, right),
        (east.at[last], west_speed, right),
        (kappa.at[last], west_kappa, right),
        (depth, west_depth, right),
        (tracer.at[:, 0], east_tracer, left),
        (kappa.at[0], east_kappa, left),
        (depth, east_depth, left),
    ]
    copies = []
    for index, (source, target, device) in enumerate(plan):
        copies.append(pltpu.make_async_remote_copy(
            src_ref=source, dst_ref=target, send_sem=out_sems.at[index],
            recv_sem=in_sems.at[index], device_id={"lon": device},
            device_id_type=pl.DeviceIdType.MESH))
        copies[-1].start()

    def pair(to, arriving):
        return pltpu.make_async_remote_copy(
            src_ref=send.at[to], dst_ref=received.at[me], send_sem=pair_out.at[to],
            recv_sem=pair_in.at[arriving], device_id={"lon": to},
            device_id_type=pl.DeviceIdType.MESH)

    @pl.loop(1, tiles)
    def _(step):
        pair(lax.rem(me + step, tiles), me).start()

    own = pltpu.make_async_copy(send.at[me], received.at[me], own_sem)
    own.start()
    own.wait()
    for copy in copies:
        copy.wait()

    @pl.loop(1, tiles)
    def _(step):
        other = lax.rem(me + step, tiles)
        pltpu.make_async_remote_copy(
            src_ref=send.at[other], dst_ref=received.at[other], send_sem=pair_out.at[other],
            recv_sem=pair_in.at[other], device_id={"lon": other},
            device_id_type=pl.DeviceIdType.MESH).wait()


def advance(tracer, east, north, kappa, mixing, thickness, depth,
            west_tracer, west_speed, west_kappa, west_depth, east_tracer, east_kappa, east_depth,
            mirror, mirror_depth, received, out, values, thick, blend, gains):
    count, lon_cells, levels = tracer.shape[:3]
    tiles = received.shape[0]
    last = lon_cells - 1

    surface = jnp.zeros((3 * count * lon_cells, LANES), F32)
    for s in range(tiles):
        rows = received[s]
        hit = iota((lon_cells, LANES), 0).astype(F32) == rows[count:count + 1]
        lines = [p[n:n + 1] for p in thirds(rows[:count]) for n in range(count)]
        spread = jnp.concatenate(
            [jnp.where(hit, line, 0.0).astype(BF16) for line in lines], axis=0)
        spots = (iota((LANES, LANES), 0).astype(F32) == rows[count + 1:count + 2]).astype(F32)
        surface = surface + lax.dot_general(
            spread, spots.astype(BF16), (((1,), (1,)), ((), ())), preferred_element_type=F32)

    def flux_of(n):
        block = [surface[(p * count + n) * lon_cells:(p * count + n + 1) * lon_cells]
                 for p in range(3)]
        return block[0] + (block[1] + block[2])

    def weights(speed, near, far, open_face):
        half = 0.5 * (near + far)
        return (jnp.where(open_face, jnp.maximum(speed, 0.0) + half, 0.0),
                jnp.where(open_face, jnp.minimum(speed, 0.0) - half, 0.0))

    for start in range(0, levels, ROWS):
        size = min(ROWS, levels - start)
        ks = pl.ds(start, size)
        level = iota((size, LANES), 0) + start
        lane = iota((size, LANES), 1)
        at_fold = lane == LANES - 1
        row_fold = iota((1, LANES), 1) == LANES - 1

        def cell(i, east_far, kappa_far, depth_far, flux_before):
            here = [tracer[n, i, ks, :] for n in range(count)]
            kappa_here = kappa[i, ks, :]
            depth_here = depth[pl.ds(i, 1), :]
            ea, eb = weights(east[i, ks, :], kappa_here, kappa_far,
                             level < jnp.minimum(depth_here, depth_far))

            def beyond(x, f):
                other = pltpu.roll(mirror[ks, :], LANES - 1 - f * lon_cells - (last - i), 1)
                return jnp.where(at_fold, other, pltpu.roll(x, LANES - 1, 1))

            speed = north[i, ks, :]
            speed_far = pltpu.roll(mirror[ks, :], LANES - 1 - count * lon_cells - (last - i), 1)
            speed = jnp.where(at_fold, 0.5 * (speed - speed_far), speed)
            depth_north = jnp.where(row_fold, mirror_depth[pl.ds(last - i, 1), :],
                                    pltpu.roll(depth_here, LANES - 1, 1))
            na, nb = weights(speed, kappa_here, beyond(kappa_here, count + 1),
                             level < jnp.minimum(depth_here, depth_north))
            layer = thickness[i, ks, :]
            spots = pl.ds(start * lon_cells + i, size, stride=lon_cells)
            thick[spots, :] = layer
            blend[spots, :] = mixing[i, ks, :]
            fluxes = []
            for n in range(count):
                flux = ea * here[n] + eb * east_far[n]
                up = na * here[n] + nb * beyond(here[n], n)
                down = jnp.where(lane == 0, 0.0, pltpu.roll(up, 1, 1))
                stepped = (here[n] - (flux - flux_before[n])) - (up - down)
                values[n, spots, :] = layer * stepped
                fluxes.append(flux)
            return tuple(fluxes)

        wa, wb = weights(west_speed[ks, :], west_kappa[ks, :], kappa[0, ks, :],
                         level < jnp.minimum(west_depth[last:last + 1, :], depth[0:1, :]))
        before = tuple(wa * west_tracer[n, ks, :] + wb * tracer[n, 0, ks, :] for n in range(count))

        def inner(i, flux_before):
            return cell(i, [tracer[n, i + 1, ks, :] for n in range(count)], kappa[i + 1, ks, :],
                        depth[pl.ds(i + 1, 1), :], flux_before)

        before = lax.fori_loop(0, last, inner, before, unroll=3)
        cell(last, [east_tracer[n, ks, :] for n in range(count)], east_kappa[ks, :],
             east_depth[0:1, :], before)

    depths = depth[...]

    def at(k):
        return pl.ds(pl.multiple_of(k * lon_cells, lon_cells), lon_cells)

    def coupled(k, here, below):
        return jnp.where(depths > k + 1, blend[at(k), :] / (0.5 * (here + below)), 0.0)

    here = thick[at(0), :]
    below = thick[at(1), :]
    coupling = coupled(0, here, below)
    scale = 1.0 / (here + coupling)
    gain = coupling * scale
    gains[at(0), :] = gain
    value = []
    for n in range(count):
        value.append((values[n, at(0), :] + jnp.where(depths > 0, flux_of(n), 0.0)) * scale)
        values[n, at(0), :] = value[n]

    def down(k, state):
        here, prior, gain, value = state
        below = thick[at(k + 1), :]
        coupling = coupled(k, here, below)
        scale = 1.0 / (here + coupling + prior - prior * gain)
        gain = coupling * scale
        gains[at(k), :] = gain
        value = tuple((values[n, at(k), :] + prior * value[n]) * scale for n in range(count))
        for n in range(count):
            values[n, at(k), :] = value[n]
        return below, coupling, gain, value

    here, prior, gain, value = lax.fori_loop(
        1, levels - 1, down, (below, coupling, gain, tuple(value)), unroll=4)
    scale = 1.0 / (here + prior - prior * gain)
    solved = []
    for n in range(count):
        solved.append((values[n, at(levels - 1), :] + prior * value[n]) * scale)
        values[n, at(levels - 1), :] = solved[n]

    def up(step, solved):
        k = levels - 2 - step
        gain = gains[at(k), :]
        solved = tuple(values[n, at(k), :] + gain * solved[n] for n in range(count))
        for n in range(count):
            values[n, at(k), :] = solved[n]
        return solved

    lax.fori_loop(0, levels - 1, up, tuple(solved), unroll=4)

    @pl.loop(0, lon_cells)
    def _(i):
        for n in range(count):
            out[n, i] = values[n, pl.ds(i, levels, stride=lon_cells), :]


def shards(tracer, east_speed, north_speed, diffusivity, mixing, thickness, depth_levels,
           air_flux, margin_tile, margin_source, margin_cell, margin_weight):
    count, lon_cells, levels, lat_cells = tracer.shape
    tiles = lax.axis_size("lon")
    records = margin_source.shape[0]
    assert lat_cells == LANES and (count + 2) * lon_cells <= LANES
    shape = jax.ShapeDtypeStruct
    vmem = pl.BlockSpec(memory_space=pltpu.VMEM)
    left_in_place = pl.BlockSpec(memory_space=pl.ANY)
    big = pltpu.CompilerParams(vmem_limit_bytes=48 << 20)

    top, send = pl.pallas_call(
        lambda *refs: prepare(tiles, *refs),
        out_shape=(shape((levels, LANES), F32), shape((tiles, 8, LANES), F32)),
        in_specs=[vmem] * 8, out_specs=(vmem, vmem), compiler_params=big, name="prepare",
    )(margin_tile.reshape(1, records), margin_source.reshape(1, records),
      margin_cell.reshape(1, records), margin_weight.reshape(1, records), air_flux,
      tracer, north_speed, diffusivity)

    column = shape((levels, LANES), F32)
    stack = shape((count, levels, LANES), F32)
    depths = shape((lon_cells, LANES), I32)
    arrived = pl.pallas_call(
        lambda *refs: exchange(tiles, *refs),
        out_shape=(stack, column, column, depths, stack, column, depths, column, depths,
                   shape((tiles, 8, LANES), F32)),
        in_specs=[left_in_place] * 6, out_specs=(left_in_place,) * 10,
        scratch_shapes=[pltpu.SemaphoreType.DMA((9,)), pltpu.SemaphoreType.DMA((9,)),
                        pltpu.SemaphoreType.DMA((tiles,)), pltpu.SemaphoreType.DMA((tiles,)),
                        pltpu.SemaphoreType.DMA],
        compiler_params=pltpu.CompilerParams(collective_id=0, has_side_effects=True),
        name="exchange",
    )(tracer, east_speed, diffusivity, depth_levels, top, send)

    flat = (levels * lon_cells, LANES)
    return pl.pallas_call(
        advance,
        out_shape=shape(tracer.shape, F32),
        in_specs=[vmem] * 17, out_specs=vmem,
        scratch_shapes=[pltpu.VMEM((count, *flat), F32), pltpu.VMEM(flat, F32),
                        pltpu.VMEM(flat, F32), pltpu.VMEM(flat, F32)],
        compiler_params=big, name="advance",
    )(tracer, east_speed, north_speed, diffusivity, mixing, thickness, depth_levels, *arrived)


def solution(mesh):
    placed = (
        P(None, "lon", None, "ens"),
        P("lon", None, "ens"),
        P("lon", None, "ens"),
        P("lon", None, "ens"),
        P("lon", None, "ens"),
        P("lon", None, "ens"),
        P("lon", "ens"),
        P("ens", "lon"),
        P(("ens", "lon"), None),
        P(("ens", "lon")),
        P(("ens", "lon")),
        P(("ens", "lon")),
    )
    return jax.shard_map(
        shards, mesh=mesh, in_specs=placed, out_specs=P(None, "lon", None, "ens"), check_vma=False
    )
```

```python
import jax
import jax.numpy as jnp
from jax import lax
from jax.experimental import pallas as pl
from jax.experimental.pallas import tpu as pltpu
from jax.sharding import PartitionSpec as P

CAP = 64
LANES = 128
F32 = jnp.float32
BF16 = jnp.bfloat16
I32 = jnp.int32


def iota(shape, axis):
    return lax.broadcasted_iota(I32, shape, axis)


def thirds(x):
    high = x.astype(BF16).astype(F32)
    rest = x - high
    middle = rest.astype(BF16).astype(F32)
    return high, middle, rest - middle


def route(tiles, tile, source, cells, weight, air, send_ref):
    count, air_cells = air.shape
    records = tile.shape[1]
    picks = (iota((air_cells, records), 0) == source).astype(F32).astype(BF16)
    parts = jnp.concatenate(thirds(air), axis=0).astype(BF16)
    found = jnp.dot(parts, picks, preferred_element_type=F32)
    found = found[:count] + (found[count:2 * count] + found[2 * count:])
    payload = weight * found

    chosen = (iota((tiles, records), 0) == tile).astype(F32)
    earlier = (iota((LANES, LANES), 0) < iota((LANES, LANES), 1)).astype(F32).astype(BF16)
    carried = jnp.zeros((tiles, 1), F32)
    slots = []
    for start in range(0, records, LANES):
        piece = chosen[:, start:start + LANES]
        rank = jnp.dot(piece.astype(BF16), earlier, preferred_element_type=F32) + carried
        slots.append(jnp.sum(piece * rank, axis=0, keepdims=True))
        carried = carried + jnp.sum(piece, axis=1, keepdims=True)
    slot = jnp.concatenate(slots, axis=1)
    places = (iota((CAP, records), 0).astype(F32) == slot).astype(F32).astype(BF16)

    row = (cells >> 7).astype(F32)
    column = (cells & (LANES - 1)).astype(F32)
    lines = [p[n:n + 1] for p in thirds(payload) for n in range(count)] + [row, column]
    spread = jnp.concatenate([(chosen * line).astype(BF16) for line in lines], axis=0)
    packed = lax.dot_general(spread, places, (((1,), (1,)), ((), ())), preferred_element_type=F32)

    def part(index):
        return packed[index * tiles:(index + 1) * tiles]

    send_ref[...] = jnp.zeros(send_ref.shape, F32)
    for n in range(count):
        send_ref[:, n, :CAP] = part(n) + (part(count + n) + part(2 * count + n))
    send_ref[:, count, :CAP] = part(3 * count)
    send_ref[:, count + 1, :CAP] = part(3 * count + 1)


def gathered(received, count, lon_cells):
    surface = jnp.zeros((3 * count * lon_cells, LANES), F32)
    for s in range(received.shape[0]):
        rows = received[s]
        hit = iota((lon_cells, LANES), 0).astype(F32) == rows[count:count + 1]
        lines = [p[n:n + 1] for p in thirds(rows[:count]) for n in range(count)]
        spread = jnp.concatenate(
            [jnp.where(hit, line, 0.0).astype(BF16) for line in lines], axis=0)
        spots = (iota((LANES, LANES), 0).astype(F32) == rows[count + 1:count + 2]).astype(F32)
        surface = surface + lax.dot_general(
            spread, spots.astype(BF16), (((1,), (1,)), ((), ())), preferred_element_type=F32)
    fluxes = []
    for n in range(count):
        block = [surface[(p * count + n) * lon_cells:(p * count + n + 1) * lon_cells]
                 for p in range(3)]
        fluxes.append(block[0] + (block[1] + block[2]))
    return fluxes


def weights(speed, near, far, open_face):
    half = 0.5 * (near + far)
    return (jnp.where(open_face, jnp.maximum(speed, 0.0) + half, 0.0),
            jnp.where(open_face, jnp.minimum(speed, 0.0) - half, 0.0))


def step(tiles, *refs):
    sources, refs = refs[:12], refs[12:]
    out, refs = refs[0], refs[1:]
    held, refs = refs[:12], refs[12:]
    (values, gains, factor, share, top, fold_out, fold_in, right_out, right_in, left_out, left_in,
     send, received, load_sems, store_sems, out_sems, in_sems, pair_out, pair_in, own_sem) = refs
    (tracer, east, north, kappa, mixing, thickness, depth_ref, air, tile, source, cells,
     weight) = held
    count, planes = tracer.shape[:2]
    lon_cells = depth_ref.shape[0]
    levels = planes // lon_cells
    last = lon_cells - 1

    loads = [pltpu.make_async_copy(a, b, load_sems.at[i])
             for i, (a, b) in enumerate(zip(sources, held))]
    for i in (7, 8, 9, 10, 11, 0, 2, 3, 1, 6, 5, 4):
        loads[i].start()

    me = lax.axis_index("lon")
    right = lax.rem(me + 1, tiles)
    left = lax.rem(me + tiles - 1, tiles)
    partner = tiles - 1 - me
    barrier = pltpu.get_barrier_semaphore()

    @pl.loop(1, tiles)
    def _(hop):
        pl.semaphore_signal(barrier, inc=1, device_id={"lon": lax.rem(me + hop, tiles)},
                            device_id_type=pl.DeviceIdType.MESH)

    for i in (7, 8, 9, 10, 11):
        loads[i].wait()
    route(tiles, tile[...], source[...], cells[...], weight[...], air[...], send)

    for i in (0, 2, 3, 1, 6):
        loads[i].wait()
    depth = depth_ref[...]

    def at(k):
        return pl.ds(pl.multiple_of(k * lon_cells, lon_cells), lon_cells)

    def column(i):
        return pl.ds(i, levels, stride=lon_cells)

    for n in range(count):
        right_out[n, :levels, :] = tracer[n, column(last), :]
        left_out[n, :levels, :] = tracer[n, column(0), :]
    right_out[count, :levels, :] = kappa[column(last), :]
    left_out[count, :levels, :] = kappa[column(0), :]
    right_out[count + 1, :levels, :] = east[column(last), :]
    right_out[count, levels:levels + 1, :] = depth[last:, :].astype(F32)
    left_out[count, levels:levels + 1, :] = depth[:1, :].astype(F32)

    lane = iota((lon_cells, LANES), 1)

    def take(k, packed):
        fields = [tracer[n, at(k), :] for n in range(count)] + [kappa[at(k), :], north[at(k), :]]
        return tuple(jnp.where(lane == k, pltpu.roll(x, k + 1, 1), p)
                     for x, p in zip(fields, packed))

    empty = jnp.zeros((lon_cells, LANES), F32)
    packed = lax.fori_loop(0, levels, take, (empty,) * (count + 2), unroll=3)
    packed += (jnp.broadcast_to(depth[:, LANES - 1:].astype(F32), (lon_cells, LANES)),)
    for f, plane in enumerate(packed):
        top[f] = plane
        for i in range(lon_cells):
            fold_out[f, last - i:last - i + 1, :] = plane[i:i + 1]

    pl.semaphore_wait(barrier, tiles - 1)
    copies = []
    for index, (a, b, device) in enumerate([
            (right_out, right_in, right), (left_out, left_in, left), (fold_out, fold_in, partner)]):
        copies.append(pltpu.make_async_remote_copy(
            src_ref=a, dst_ref=b, send_sem=out_sems.at[index], recv_sem=in_sems.at[index],
            device_id={"lon": device}, device_id_type=pl.DeviceIdType.MESH))
        copies[-1].start()

    @pl.loop(1, tiles)
    def _(hop):
        other = lax.rem(me + hop, tiles)
        pltpu.make_async_remote_copy(
            src_ref=send.at[other], dst_ref=received.at[me], send_sem=pair_out.at[other],
            recv_sem=pair_in.at[me], device_id={"lon": other},
            device_id_type=pl.DeviceIdType.MESH).start()

    own = pltpu.make_async_copy(send.at[me], received.at[me], own_sem)
    own.start()
    for i in (5, 4):
        loads[i].wait()

    row = iota((lon_cells, LANES), 0)
    depth_east = jnp.where(row == last, 0, pltpu.roll(depth, last, 0))
    depth_north = jnp.where(lane == LANES - 1, 0, pltpu.roll(depth, LANES - 1, 1))
    open_east = jnp.minimum(depth, depth_east)
    open_north = jnp.minimum(depth, depth_north)

    def inner(k, state):
        prior, gain = state
        here = thickness[at(k), :]
        below = thickness[at(jnp.minimum(k + 1, levels - 1)), :]
        coupling = jnp.where(depth > k + 1, mixing[at(k), :] / (0.5 * (here + below)), 0.0)
        scale = 1.0 / (here + coupling + prior - prior * gain)
        gain = coupling * scale
        gains[at(k), :] = gain
        factor[at(k), :] = prior * scale
        part = here * scale
        share[at(k), :] = part
        spread = kappa[at(k), :]
        ea, eb = weights(east[at(k), :], spread, pltpu.roll(spread, last, 0), open_east > k)
        na, nb = weights(north[at(k), :], spread, pltpu.roll(spread, LANES - 1, 1), open_north > k)
        for n in range(count):
            t = tracer[n, at(k), :]
            zonal = ea * t + eb * pltpu.roll(t, last, 0)
            up = na * t + nb * pltpu.roll(t, LANES - 1, 1)
            stepped = (t - (zonal - pltpu.roll(zonal, 1, 0))) - (up - pltpu.roll(up, 1, 1))
            values[n, at(k), :] = part * stepped
        return coupling, gain

    lax.fori_loop(0, levels, inner, (empty, empty), unroll=3)

    for copy in copies:
        copy.wait()
    deep = iota((levels, LANES), 0)

    first_share = share[column(0), :]
    last_share = share[column(last), :]
    wa, wb = weights(right_in[count + 1, :levels, :], right_in[count, :levels, :],
                     kappa[column(0), :],
                     deep < jnp.minimum(right_in[count, levels:levels + 1, :].astype(I32), depth[:1]))
    ea, eb = weights(east[column(last), :], kappa[column(last), :], left_in[count, :levels, :],
                     deep < jnp.minimum(left_in[count, levels:levels + 1, :].astype(I32), depth[last:]))
    for n in range(count):
        flux = wa * right_in[n, :levels, :] + wb * tracer[n, column(0), :]
        values[n, column(0), :] = values[n, column(0), :] + first_share * flux
        flux = ea * tracer[n, column(last), :] + eb * left_in[n, :levels, :]
        values[n, column(last), :] = values[n, column(last), :] - last_share * flux
    fa, fb = weights(0.5 * (top[count + 1] - fold_in[count + 1]), top[count], fold_in[count],
                     lane < jnp.minimum(top[count + 2], fold_in[count + 2]).astype(I32))
    fold = [fa * top[n] + fb * fold_in[n] for n in range(count)]

    own.wait()

    @pl.loop(1, tiles)
    def _(hop):
        other = lax.rem(me + hop, tiles)
        pltpu.make_async_remote_copy(
            src_ref=send.at[other], dst_ref=received.at[other], send_sem=pair_out.at[other],
            recv_sem=pair_in.at[other], device_id={"lon": other},
            device_id_type=pl.DeviceIdType.MESH).wait()

    surface = gathered(received, count, lon_cells)
    pivot = share[at(0), :] / thickness[at(0), :]
    for n in range(count):
        values[n, at(0), :] = values[n, at(0), :] + jnp.where(depth > 0, surface[n] * pivot, 0.0)

    def down(k, value):
        part = jnp.where(lane == LANES - 1, share[at(k), :], 0.0)
        mult = factor[at(k), :]
        solved = []
        for n in range(count):
            own_part = values[n, at(k), :] - part * pltpu.roll(fold[n], LANES - 1 - k, 1)
            solved.append(own_part + mult * value[n])
            values[n, at(k), :] = solved[n]
        return tuple(solved)

    value = lax.fori_loop(0, levels, down, (empty,) * count, unroll=3)

    chunk = 15
    stores = []
    value = (empty,) * count
    for index, begin in enumerate(range(levels // chunk * chunk, -1, -chunk)):
        end = min(begin + chunk, levels)
        if begin == end:
            continue

        def up(move, value, end=end):
            k = end - 1 - move
            gain = gains[at(k), :]
            solved = tuple(values[n, at(k), :] + gain * value[n] for n in range(count))
            for n in range(count):
                values[n, at(k), :] = solved[n]
            return solved

        value = lax.fori_loop(0, end - begin, up, value, unroll=5)
        block = pl.ds(begin * lon_cells, (end - begin) * lon_cells)
        stores.append(pltpu.make_async_copy(
            values.at[:, block], out.at[:, block], store_sems.at[index]))
        stores[-1].start()
    for store in stores:
        store.wait()


def shards(tracer, east_speed, north_speed, diffusivity, mixing, thickness, depth_levels,
           air_flux, margin_tile, margin_source, margin_cell, margin_weight):
    count, lon_cells, levels, lat_cells = tracer.shape
    tiles = lax.axis_size("lon")
    records = margin_source.shape[0]
    assert lat_cells == LANES and levels < LANES

    def by_level(x):
        return x.transpose(1, 0, 2).reshape(levels * lon_cells, LANES)

    operands = (
        tracer.transpose(0, 2, 1, 3).reshape(count, levels * lon_cells, LANES),
        *[by_level(x) for x in (east_speed, north_speed, diffusivity, mixing, thickness)],
        depth_levels, air_flux,
        *[x.reshape(1, records) for x in (margin_tile, margin_source, margin_cell, margin_weight)])
    hbm = pl.BlockSpec(memory_space=pltpu.HBM)
    flat = pltpu.VMEM((levels * lon_cells, LANES), F32)
    rows = (levels + 8) // 8 * 8
    fold = pltpu.VMEM((count + 3, lon_cells, LANES), F32)
    pairs = pltpu.VMEM((tiles, 8, LANES), F32)
    dma = pltpu.SemaphoreType.DMA
    result = pl.pallas_call(
        lambda *refs: step(tiles, *refs),
        out_shape=jax.ShapeDtypeStruct(operands[0].shape, F32),
        in_specs=[hbm] * 12, out_specs=hbm,
        scratch_shapes=[pltpu.VMEM(x.shape, x.dtype) for x in operands] + [
            pltpu.VMEM(operands[0].shape, F32), flat, flat, flat, fold, fold, fold,
            pltpu.VMEM((count + 2, rows, LANES), F32), pltpu.VMEM((count + 2, rows, LANES), F32),
            pltpu.VMEM((count + 1, rows, LANES), F32), pltpu.VMEM((count + 1, rows, LANES), F32),
            pairs, pairs, dma((12,)), dma((levels // 15 + 1,)), dma((3,)), dma((3,)),
            dma((tiles,)), dma((tiles,)), dma],
        compiler_params=pltpu.CompilerParams(
            collective_id=0, has_side_effects=True, vmem_limit_bytes=60 << 20),
        name="ocean_step",
    )(*operands)
    return result.reshape(count, levels, lon_cells, LANES).transpose(0, 2, 1, 3)


def solution(mesh):
    placed = (
        P(None, "lon", None, "ens"),
        P("lon", None, "ens"),
        P("lon", None, "ens"),
        P("lon", None, "ens"),
        P("lon", None, "ens"),
        P("lon", None, "ens"),
        P("lon", "ens"),
        P("ens", "lon"),
        P(("ens", "lon"), None),
        P(("ens", "lon")),
        P(("ens", "lon")),
        P(("ens", "lon")),
    )
    return jax.shard_map(
        shards, mesh=mesh, in_specs=placed, out_specs=P(None, "lon", None, "ens"), check_vma=False
    )
```

```python
import jax
import jax.numpy as jnp
from jax import lax
from jax.experimental import pallas as pl
from jax.experimental.pallas import tpu as pltpu
from jax.sharding import PartitionSpec as P

CAP = 64
LANES = 128
F32 = jnp.float32
BF16 = jnp.bfloat16
I32 = jnp.int32


def iota(shape, axis):
    return lax.broadcasted_iota(I32, shape, axis)


def thirds(x):
    high = x.astype(BF16).astype(F32)
    rest = x - high
    middle = rest.astype(BF16).astype(F32)
    return high, middle, rest - middle


def route(tiles, tile, source, cells, weight, air, send_ref):
    count, air_cells = air.shape
    records = tile.shape[1]
    picks = (iota((air_cells, records), 0) == source).astype(F32).astype(BF16)
    parts = jnp.concatenate(thirds(air), axis=0).astype(BF16)
    found = jnp.dot(parts, picks, preferred_element_type=F32)
    found = found[:count] + (found[count:2 * count] + found[2 * count:])
    payload = weight * found

    chosen = (iota((tiles, records), 0) == tile).astype(F32)
    earlier = (iota((LANES, LANES), 0) < iota((LANES, LANES), 1)).astype(F32).astype(BF16)
    carried = jnp.zeros((tiles, 1), F32)
    slots = []
    for start in range(0, records, LANES):
        piece = chosen[:, start:start + LANES]
        rank = jnp.dot(piece.astype(BF16), earlier, preferred_element_type=F32) + carried
        slots.append(jnp.sum(piece * rank, axis=0, keepdims=True))
        carried = carried + jnp.sum(piece, axis=1, keepdims=True)
    slot = jnp.concatenate(slots, axis=1)
    places = (iota((CAP, records), 0).astype(F32) == slot).astype(F32).astype(BF16)

    row = (cells >> 7).astype(F32)
    column = (cells & (LANES - 1)).astype(F32)
    lines = [p[n:n + 1] for p in thirds(payload) for n in range(count)] + [row, column]
    spread = jnp.concatenate([(chosen * line).astype(BF16) for line in lines], axis=0)
    packed = lax.dot_general(spread, places, (((1,), (1,)), ((), ())), preferred_element_type=F32)

    def part(index):
        return packed[index * tiles:(index + 1) * tiles]

    send_ref[...] = jnp.zeros(send_ref.shape, F32)
    for n in range(count):
        send_ref[:, n, :CAP] = part(n) + (part(count + n) + part(2 * count + n))
    send_ref[:, count, :CAP] = part(3 * count)
    send_ref[:, count + 1, :CAP] = part(3 * count + 1)


def gathered(received, count, lon_cells):
    surface = jnp.zeros((3 * count * lon_cells, LANES), F32)
    for s in range(received.shape[0]):
        rows = received[s]
        hit = iota((lon_cells, LANES), 0).astype(F32) == rows[count:count + 1]
        lines = [p[n:n + 1] for p in thirds(rows[:count]) for n in range(count)]
        spread = jnp.concatenate(
            [jnp.where(hit, line, 0.0).astype(BF16) for line in lines], axis=0)
        spots = (iota((LANES, LANES), 0).astype(F32) == rows[count + 1:count + 2]).astype(F32)
        surface = surface + lax.dot_general(
            spread, spots.astype(BF16), (((1,), (1,)), ((), ())), preferred_element_type=F32)
    fluxes = []
    for n in range(count):
        block = [surface[(p * count + n) * lon_cells:(p * count + n + 1) * lon_cells]
                 for p in range(3)]
        fluxes.append(block[0] + (block[1] + block[2]))
    return fluxes


def weights(speed, near, far, open_face):
    half = 0.5 * (near + far)
    return (jnp.where(open_face, jnp.maximum(speed, 0.0) + half, 0.0),
            jnp.where(open_face, jnp.minimum(speed, 0.0) - half, 0.0))


def step(tiles, *refs):
    sources, refs = refs[:12], refs[12:]
    out, refs = refs[0], refs[1:]
    held, refs = refs[:12], refs[12:]
    (values, gains, factor, share, top, fold_out, fold_in, right_out, right_in, left_out, left_in,
     send, received, load_sems, store_sems, out_sems, in_sems, pair_out, pair_in, own_sem) = refs
    (tracer, east, north, kappa, mixing, thickness, depth_ref, air, tile, source, cells,
     weight) = held
    count, planes = tracer.shape[:2]
    lon_cells = depth_ref.shape[0]
    levels = planes // lon_cells
    last = lon_cells - 1

    loads = [pltpu.make_async_copy(a, b, load_sems.at[i])
             for i, (a, b) in enumerate(zip(sources, held))]
    for i in (7, 8, 9, 10, 11, 0, 2, 3, 1, 6, 5, 4):
        loads[i].start()

    me = lax.axis_index("lon")
    right = lax.rem(me + 1, tiles)
    left = lax.rem(me + tiles - 1, tiles)
    partner = tiles - 1 - me
    barrier = pltpu.get_barrier_semaphore()

    @pl.loop(1, tiles)
    def _(hop):
        pl.semaphore_signal(barrier, inc=1, device_id={"lon": lax.rem(me + hop, tiles)},
                            device_id_type=pl.DeviceIdType.MESH)

    for i in (7, 8, 9, 10, 11):
        loads[i].wait()
    route(tiles, tile[...], source[...], cells[...], weight[...], air[...], send)

    for i in (0, 2, 3, 1, 6):
        loads[i].wait()
    depth = depth_ref[...]

    def at(k):
        return pl.ds(pl.multiple_of(k * lon_cells, lon_cells), lon_cells)

    def column(i):
        return pl.ds(i, levels, stride=lon_cells)

    for n in range(count):
        right_out[n, :levels, :] = tracer[n, column(last), :]
        left_out[n, :levels, :] = tracer[n, column(0), :]
    right_out[count, :levels, :] = kappa[column(last), :]
    left_out[count, :levels, :] = kappa[column(0), :]
    right_out[count + 1, :levels, :] = east[column(last), :]
    right_out[count, levels:levels + 1, :] = depth[last:, :].astype(F32)
    left_out[count, levels:levels + 1, :] = depth[:1, :].astype(F32)

    pl.semaphore_wait(barrier, tiles - 1)
    copies = []

    def start(a, b, device):
        index = len(copies)
        copies.append(pltpu.make_async_remote_copy(
            src_ref=a, dst_ref=b, send_sem=out_sems.at[index], recv_sem=in_sems.at[index],
            device_id={"lon": device}, device_id_type=pl.DeviceIdType.MESH))
        copies[-1].start()

    start(right_out, right_in, right)
    start(left_out, left_in, left)

    @pl.loop(1, tiles)
    def _(hop):
        other = lax.rem(me + hop, tiles)
        pltpu.make_async_remote_copy(
            src_ref=send.at[other], dst_ref=received.at[me], send_sem=pair_out.at[other],
            recv_sem=pair_in.at[me], device_id={"lon": other},
            device_id_type=pl.DeviceIdType.MESH).start()

    lane = iota((lon_cells, LANES), 1)

    def take(k, packed):
        fields = [tracer[n, at(k), :] for n in range(count)] + [kappa[at(k), :], north[at(k), :]]
        return tuple(jnp.where(lane == k, pltpu.roll(x, k + 1, 1), p)
                     for x, p in zip(fields, packed))

    empty = jnp.zeros((lon_cells, LANES), F32)
    packed = lax.fori_loop(0, levels, take, (empty,) * (count + 2), unroll=15)
    packed += (jnp.broadcast_to(depth[:, LANES - 1:].astype(F32), (lon_cells, LANES)),)
    for f, plane in enumerate(packed):
        top[f] = plane
        for i in range(lon_cells):
            fold_out[f, last - i:last - i + 1, :] = plane[i:i + 1]

    start(fold_out, fold_in, partner)
    own = pltpu.make_async_copy(send.at[me], received.at[me], own_sem)
    own.start()
    for i in (5, 4):
        loads[i].wait()

    row = iota((lon_cells, LANES), 0)
    depth_east = jnp.where(row == last, 0, pltpu.roll(depth, last, 0))
    depth_north = jnp.where(lane == LANES - 1, 0, pltpu.roll(depth, LANES - 1, 1))
    open_east = jnp.minimum(depth, depth_east)
    open_north = jnp.minimum(depth, depth_north)

    def inner(k, state):
        prior, gain = state
        here = thickness[at(k), :]
        below = thickness[at(jnp.minimum(k + 1, levels - 1)), :]
        coupling = jnp.where(depth > k + 1, mixing[at(k), :] / (0.5 * (here + below)), 0.0)
        scale = 1.0 / (here + coupling + prior - prior * gain)
        gain = coupling * scale
        gains[at(k), :] = gain
        factor[at(k), :] = prior * scale
        part = here * scale
        share[at(k), :] = part
        spread = kappa[at(k), :]
        ea, eb = weights(east[at(k), :], spread, pltpu.roll(spread, last, 0), open_east > k)
        na, nb = weights(north[at(k), :], spread, pltpu.roll(spread, LANES - 1, 1), open_north > k)
        for n in range(count):
            t = tracer[n, at(k), :]
            zonal = ea * t + eb * pltpu.roll(t, last, 0)
            up = na * t + nb * pltpu.roll(t, LANES - 1, 1)
            stepped = (t - (zonal - pltpu.roll(zonal, 1, 0))) - (up - pltpu.roll(up, 1, 1))
            values[n, at(k), :] = part * stepped
        return coupling, gain

    lax.fori_loop(0, levels, inner, (empty, empty), unroll=3)

    for copy in copies:
        copy.wait()
    deep = iota((levels, LANES), 0)

    first_share = share[column(0), :]
    last_share = share[column(last), :]
    wa, wb = weights(right_in[count + 1, :levels, :], right_in[count, :levels, :],
                     kappa[column(0), :],
                     deep < jnp.minimum(right_in[count, levels:levels + 1, :].astype(I32), depth[:1]))
    ea, eb = weights(east[column(last), :], kappa[column(last), :], left_in[count, :levels, :],
                     deep < jnp.minimum(left_in[count, levels:levels + 1, :].astype(I32), depth[last:]))
    for n in range(count):
        flux = wa * right_in[n, :levels, :] + wb * tracer[n, column(0), :]
        values[n, column(0), :] = values[n, column(0), :] + first_share * flux
        flux = ea * tracer[n, column(last), :] + eb * left_in[n, :levels, :]
        values[n, column(last), :] = values[n, column(last), :] - last_share * flux
    fa, fb = weights(0.5 * (top[count + 1] - fold_in[count + 1]), top[count], fold_in[count],
                     lane < jnp.minimum(top[count + 2], fold_in[count + 2]).astype(I32))
    fold = [fa * top[n] + fb * fold_in[n] for n in range(count)]

    own.wait()

    @pl.loop(1, tiles)
    def _(hop):
        other = lax.rem(me + hop, tiles)
        pltpu.make_async_remote_copy(
            src_ref=send.at[other], dst_ref=received.at[other], send_sem=pair_out.at[other],
            recv_sem=pair_in.at[other], device_id={"lon": other},
            device_id_type=pl.DeviceIdType.MESH).wait()

    surface = gathered(received, count, lon_cells)
    pivot = share[at(0), :] / thickness[at(0), :]
    for n in range(count):
        values[n, at(0), :] = values[n, at(0), :] + jnp.where(depth > 0, surface[n] * pivot, 0.0)

    def down(k, value):
        part = jnp.where(lane == LANES - 1, share[at(k), :], 0.0)
        mult = factor[at(k), :]
        solved = []
        for n in range(count):
            own_part = values[n, at(k), :] - part * pltpu.roll(fold[n], LANES - 1 - k, 1)
            solved.append(own_part + mult * value[n])
            values[n, at(k), :] = solved[n]
        return tuple(solved)

    value = lax.fori_loop(0, levels, down, (empty,) * count, unroll=15)

    chunk = 15
    stores = []
    value = (empty,) * count
    for index, begin in enumerate(range(levels // chunk * chunk, -1, -chunk)):
        end = min(begin + chunk, levels)
        if begin == end:
            continue

        def up(move, value, end=end):
            k = end - 1 - move
            gain = gains[at(k), :]
            solved = tuple(values[n, at(k), :] + gain * value[n] for n in range(count))
            for n in range(count):
                values[n, at(k), :] = solved[n]
            return solved

        value = lax.fori_loop(0, end - begin, up, value, unroll=15)
        block = pl.ds(begin * lon_cells, (end - begin) * lon_cells)
        stores.append(pltpu.make_async_copy(
            values.at[:, block], out.at[:, block], store_sems.at[index]))
        stores[-1].start()
    for store in stores:
        store.wait()


def shards(tracer, east_speed, north_speed, diffusivity, mixing, thickness, depth_levels,
           air_flux, margin_tile, margin_source, margin_cell, margin_weight):
    count, lon_cells, levels, lat_cells = tracer.shape
    tiles = lax.axis_size("lon")
    records = margin_source.shape[0]
    assert lat_cells == LANES and levels < LANES

    def by_level(x):
        return x.transpose(1, 0, 2).reshape(levels * lon_cells, LANES)

    operands = (
        tracer.transpose(0, 2, 1, 3).reshape(count, levels * lon_cells, LANES),
        *[by_level(x) for x in (east_speed, north_speed, diffusivity, mixing, thickness)],
        depth_levels, air_flux,
        *[x.reshape(1, records) for x in (margin_tile, margin_source, margin_cell, margin_weight)])
    hbm = pl.BlockSpec(memory_space=pltpu.HBM)
    flat = pltpu.VMEM((levels * lon_cells, LANES), F32)
    rows = (levels + 8) // 8 * 8
    fold = pltpu.VMEM((count + 3, lon_cells, LANES), F32)
    pairs = pltpu.VMEM((tiles, 8, LANES), F32)
    dma = pltpu.SemaphoreType.DMA
    result = pl.pallas_call(
        lambda *refs: step(tiles, *refs),
        out_shape=jax.ShapeDtypeStruct(operands[0].shape, F32),
        in_specs=[hbm] * 12, out_specs=hbm,
        scratch_shapes=[pltpu.VMEM(x.shape, x.dtype) for x in operands] + [
            pltpu.VMEM(operands[0].shape, F32), flat, flat, flat, fold, fold, fold,
            pltpu.VMEM((count + 2, rows, LANES), F32), pltpu.VMEM((count + 2, rows, LANES), F32),
            pltpu.VMEM((count + 1, rows, LANES), F32), pltpu.VMEM((count + 1, rows, LANES), F32),
            pairs, pairs, dma((12,)), dma((levels // 15 + 1,)), dma((3,)), dma((3,)),
            dma((tiles,)), dma((tiles,)), dma],
        compiler_params=pltpu.CompilerParams(
            collective_id=0, has_side_effects=True, vmem_limit_bytes=60 << 20),
        name="ocean_step",
    )(*operands)
    return result.reshape(count, levels, lon_cells, LANES).transpose(0, 2, 1, 3)


def solution(mesh):
    placed = (
        P(None, "lon", None, "ens"),
        P("lon", None, "ens"),
        P("lon", None, "ens"),
        P("lon", None, "ens"),
        P("lon", None, "ens"),
        P("lon", None, "ens"),
        P("lon", "ens"),
        P("ens", "lon"),
        P(("ens", "lon"), None),
        P(("ens", "lon")),
        P(("ens", "lon")),
        P(("ens", "lon")),
    )
    return jax.shard_map(
        shards, mesh=mesh, in_specs=placed, out_specs=P(None, "lon", None, "ens"), check_vma=False
    )
```

```python
import jax
import jax.numpy as jnp
from jax import lax
from jax.experimental import pallas as pl
from jax.experimental.pallas import tpu as pltpu
from jax.sharding import PartitionSpec as P

CAP = 64
CHUNK = 15
LANES = 128
F32 = jnp.float32
BF16 = jnp.bfloat16
I32 = jnp.int32


def iota(shape, axis):
    return lax.broadcasted_iota(I32, shape, axis)


def thirds(x):
    high = x.astype(BF16).astype(F32)
    rest = x - high
    middle = rest.astype(BF16).astype(F32)
    return high, middle, rest - middle


def route(tiles, tile, source, cells, weight, air, send_ref):
    count, air_cells = air.shape
    records = tile.shape[1]
    picks = (iota((air_cells, records), 0) == source).astype(F32).astype(BF16)
    parts = jnp.concatenate(thirds(air), axis=0).astype(BF16)
    found = jnp.dot(parts, picks, preferred_element_type=F32)
    found = found[:count] + (found[count:2 * count] + found[2 * count:])
    payload = weight * found

    chosen = (iota((tiles, records), 0) == tile).astype(F32)
    earlier = (iota((LANES, LANES), 0) < iota((LANES, LANES), 1)).astype(F32).astype(BF16)
    carried = jnp.zeros((tiles, 1), F32)
    slots = []
    for start in range(0, records, LANES):
        piece = chosen[:, start:start + LANES]
        rank = jnp.dot(piece.astype(BF16), earlier, preferred_element_type=F32) + carried
        slots.append(jnp.sum(piece * rank, axis=0, keepdims=True))
        carried = carried + jnp.sum(piece, axis=1, keepdims=True)
    slot = jnp.concatenate(slots, axis=1)
    places = (iota((CAP, records), 0).astype(F32) == slot).astype(F32).astype(BF16)

    row = (cells >> 7).astype(F32)
    column = (cells & (LANES - 1)).astype(F32)
    lines = [p[n:n + 1] for p in thirds(payload) for n in range(count)] + [row, column]
    spread = jnp.concatenate([(chosen * line).astype(BF16) for line in lines], axis=0)
    packed = lax.dot_general(spread, places, (((1,), (1,)), ((), ())), preferred_element_type=F32)

    def part(index):
        return packed[index * tiles:(index + 1) * tiles]

    send_ref[...] = jnp.zeros(send_ref.shape, F32)
    for n in range(count):
        send_ref[:, n, :CAP] = part(n) + (part(count + n) + part(2 * count + n))
    send_ref[:, count, :CAP] = part(3 * count)
    send_ref[:, count + 1, :CAP] = part(3 * count + 1)


def gathered(received, count, lon_cells):
    surface = jnp.zeros((3 * count * lon_cells, LANES), F32)
    for s in range(received.shape[0]):
        rows = received[s]
        hit = iota((lon_cells, LANES), 0).astype(F32) == rows[count:count + 1]
        lines = [p[n:n + 1] for p in thirds(rows[:count]) for n in range(count)]
        spread = jnp.concatenate(
            [jnp.where(hit, line, 0.0).astype(BF16) for line in lines], axis=0)
        spots = (iota((LANES, LANES), 0).astype(F32) == rows[count + 1:count + 2]).astype(F32)
        surface = surface + lax.dot_general(
            spread, spots.astype(BF16), (((1,), (1,)), ((), ())), preferred_element_type=F32)
    fluxes = []
    for n in range(count):
        block = [surface[(p * count + n) * lon_cells:(p * count + n + 1) * lon_cells]
                 for p in range(3)]
        fluxes.append(block[0] + (block[1] + block[2]))
    return fluxes


def weights(speed, near, far, open_face):
    half = 0.5 * (near + far)
    return (jnp.where(open_face, jnp.maximum(speed, 0.0) + half, 0.0),
            jnp.where(open_face, jnp.minimum(speed, 0.0) - half, 0.0))


def step(tiles, *refs):
    sources, refs = refs[:12], refs[12:]
    values, gains, refs = refs[0], refs[1], refs[2:]
    held, refs = refs[:12], refs[12:]
    (factor, share, top, fold_out, fold_in, right_out, right_in, left_out, left_in,
     send, received, load_sems, out_sems, in_sems, pair_out, pair_in, own_sem) = refs
    (tracer, east, north, kappa, mixing, thickness, depth_ref, air, tile, source, cells,
     weight) = held
    count, planes = tracer.shape[:2]
    lon_cells = depth_ref.shape[0]
    levels = planes // lon_cells
    last = lon_cells - 1

    loads = [pltpu.make_async_copy(a, b, load_sems.at[i])
             for i, (a, b) in enumerate(zip(sources, held))]
    for i in (7, 8, 9, 10, 11, 0, 2, 3, 1, 6, 5, 4):
        loads[i].start()

    me = lax.axis_index("lon")
    right = lax.rem(me + 1, tiles)
    left = lax.rem(me + tiles - 1, tiles)
    partner = tiles - 1 - me
    barrier = pltpu.get_barrier_semaphore()

    @pl.loop(1, tiles)
    def _(hop):
        pl.semaphore_signal(barrier, inc=1, device_id={"lon": lax.rem(me + hop, tiles)},
                            device_id_type=pl.DeviceIdType.MESH)

    for i in (7, 8, 9, 10, 11):
        loads[i].wait()
    route(tiles, tile[...], source[...], cells[...], weight[...], air[...], send)

    for i in (0, 2, 3, 1, 6):
        loads[i].wait()
    depth = depth_ref[...]

    def at(k):
        return pl.ds(pl.multiple_of(k * lon_cells, lon_cells), lon_cells)

    def column(i):
        return pl.ds(i, levels, stride=lon_cells)

    for n in range(count):
        right_out[n, :levels, :] = tracer[n, column(last), :]
        left_out[n, :levels, :] = tracer[n, column(0), :]
    right_out[count, :levels, :] = kappa[column(last), :]
    left_out[count, :levels, :] = kappa[column(0), :]
    right_out[count + 1, :levels, :] = east[column(last), :]
    right_out[count, levels:levels + 1, :] = depth[last:, :].astype(F32)
    left_out[count, levels:levels + 1, :] = depth[:1, :].astype(F32)

    pl.semaphore_wait(barrier, tiles - 1)
    copies = []

    def start(a, b, device):
        index = len(copies)
        copies.append(pltpu.make_async_remote_copy(
            src_ref=a, dst_ref=b, send_sem=out_sems.at[index], recv_sem=in_sems.at[index],
            device_id={"lon": device}, device_id_type=pl.DeviceIdType.MESH))
        copies[-1].start()

    start(right_out, right_in, right)
    start(left_out, left_in, left)

    @pl.loop(1, tiles)
    def _(hop):
        other = lax.rem(me + hop, tiles)
        pltpu.make_async_remote_copy(
            src_ref=send.at[other], dst_ref=received.at[me], send_sem=pair_out.at[other],
            recv_sem=pair_in.at[me], device_id={"lon": other},
            device_id_type=pl.DeviceIdType.MESH).start()

    lane = iota((lon_cells, LANES), 1)

    def take(k, packed):
        fields = [tracer[n, at(k), :] for n in range(count)] + [kappa[at(k), :], north[at(k), :]]
        return tuple(jnp.where(lane == k, pltpu.roll(x, k + 1, 1), p)
                     for x, p in zip(fields, packed))

    empty = jnp.zeros((lon_cells, LANES), F32)
    packed = lax.fori_loop(0, levels, take, (empty,) * (count + 2), unroll=15)
    packed += (jnp.broadcast_to(depth[:, LANES - 1:].astype(F32), (lon_cells, LANES)),)
    for f, plane in enumerate(packed):
        top[f] = plane
        for i in range(lon_cells):
            fold_out[f, last - i:last - i + 1, :] = plane[i:i + 1]

    start(fold_out, fold_in, partner)
    own = pltpu.make_async_copy(send.at[me], received.at[me], own_sem)
    own.start()
    for i in (5, 4):
        loads[i].wait()

    row = iota((lon_cells, LANES), 0)
    depth_east = jnp.where(row == last, 0, pltpu.roll(depth, last, 0))
    depth_north = jnp.where(lane == LANES - 1, 0, pltpu.roll(depth, LANES - 1, 1))
    open_east = jnp.minimum(depth, depth_east)
    open_north = jnp.minimum(depth, depth_north)

    def inner(k, state):
        prior, gain = state
        here = thickness[at(k), :]
        below = thickness[at(jnp.minimum(k + 1, levels - 1)), :]
        coupling = jnp.where(depth > k + 1, mixing[at(k), :] / (0.5 * (here + below)), 0.0)
        scale = 1.0 / (here + coupling + prior - prior * gain)
        gain = coupling * scale
        gains[at(k), :] = gain
        factor[at(k), :] = prior * scale
        part = here * scale
        share[at(k), :] = part
        spread = kappa[at(k), :]
        ea, eb = weights(east[at(k), :], spread, pltpu.roll(spread, last, 0), open_east > k)
        na, nb = weights(north[at(k), :], spread, pltpu.roll(spread, LANES - 1, 1), open_north > k)
        for n in range(count):
            t = tracer[n, at(k), :]
            zonal = ea * t + eb * pltpu.roll(t, last, 0)
            up = na * t + nb * pltpu.roll(t, LANES - 1, 1)
            stepped = (t - (zonal - pltpu.roll(zonal, 1, 0))) - (up - pltpu.roll(up, 1, 1))
            values[n, at(k), :] = part * stepped
        return coupling, gain

    lax.fori_loop(0, levels, inner, (empty, empty), unroll=3)

    for copy in copies:
        copy.wait()
    deep = iota((levels, LANES), 0)

    first_share = share[column(0), :]
    last_share = share[column(last), :]
    wa, wb = weights(right_in[count + 1, :levels, :], right_in[count, :levels, :],
                     kappa[column(0), :],
                     deep < jnp.minimum(right_in[count, levels:levels + 1, :].astype(I32), depth[:1]))
    ea, eb = weights(east[column(last), :], kappa[column(last), :], left_in[count, :levels, :],
                     deep < jnp.minimum(left_in[count, levels:levels + 1, :].astype(I32), depth[last:]))
    for n in range(count):
        flux = wa * right_in[n, :levels, :] + wb * tracer[n, column(0), :]
        values[n, column(0), :] = values[n, column(0), :] + first_share * flux
        flux = ea * tracer[n, column(last), :] + eb * left_in[n, :levels, :]
        values[n, column(last), :] = values[n, column(last), :] - last_share * flux
    fa, fb = weights(0.5 * (top[count + 1] - fold_in[count + 1]), top[count], fold_in[count],
                     lane < jnp.minimum(top[count + 2], fold_in[count + 2]).astype(I32))
    fold = [fa * top[n] + fb * fold_in[n] for n in range(count)]

    own.wait()

    @pl.loop(1, tiles)
    def _(hop):
        other = lax.rem(me + hop, tiles)
        pltpu.make_async_remote_copy(
            src_ref=send.at[other], dst_ref=received.at[other], send_sem=pair_out.at[other],
            recv_sem=pair_in.at[other], device_id={"lon": other},
            device_id_type=pl.DeviceIdType.MESH).wait()

    surface = gathered(received, count, lon_cells)
    pivot = share[at(0), :] / thickness[at(0), :]
    for n in range(count):
        values[n, at(0), :] = values[n, at(0), :] + jnp.where(depth > 0, surface[n] * pivot, 0.0)

    def down(k, value):
        part = jnp.where(lane == LANES - 1, share[at(k), :], 0.0)
        mult = factor[at(k), :]
        solved = []
        for n in range(count):
            own_part = values[n, at(k), :] - part * pltpu.roll(fold[n], LANES - 1 - k, 1)
            solved.append(own_part + mult * value[n])
            values[n, at(k), :] = solved[n]
        return tuple(solved)

    value = lax.fori_loop(0, levels, down, (empty,) * count, unroll=15)


def finish(lon_cells, values, gains, out, solved, sems):
    count, planes = values.shape[:2]
    levels = planes // lon_cells

    def at(k):
        return pl.ds(pl.multiple_of(k * lon_cells, lon_cells), lon_cells)

    stores = []
    value = (jnp.zeros((lon_cells, LANES), F32),) * count
    for index, end in enumerate(range(levels, 0, -CHUNK)):
        begin = max(end - CHUNK, 0)

        def up(move, value, end=end):
            k = end - 1 - move
            gain = gains[at(k), :]
            value = tuple(values[n, at(k), :] + gain * value[n] for n in range(count))
            for n in range(count):
                solved[n, at(k), :] = value[n]
            return value

        value = lax.fori_loop(0, end - begin, up, value, unroll=CHUNK)
        block = pl.ds(begin * lon_cells, (end - begin) * lon_cells)
        stores.append(pltpu.make_async_copy(
            solved.at[:, block], out.at[:, block], sems.at[index]))
        stores[-1].start()
    for store in stores:
        store.wait()


def shards(tracer, east_speed, north_speed, diffusivity, mixing, thickness, depth_levels,
           air_flux, margin_tile, margin_source, margin_cell, margin_weight):
    count, lon_cells, levels, lat_cells = tracer.shape
    tiles = lax.axis_size("lon")
    records = margin_source.shape[0]
    assert lat_cells == LANES and levels < LANES

    def by_level(x):
        return x.transpose(1, 0, 2).reshape(levels * lon_cells, LANES)

    operands = (
        tracer.transpose(0, 2, 1, 3).reshape(count, levels * lon_cells, LANES),
        *[by_level(x) for x in (east_speed, north_speed, diffusivity, mixing, thickness)],
        depth_levels, air_flux,
        *[x.reshape(1, records) for x in (margin_tile, margin_source, margin_cell, margin_weight)])
    hbm = pl.BlockSpec(memory_space=pltpu.HBM)
    flat = pltpu.VMEM((levels * lon_cells, LANES), F32)
    rows = (levels + 8) // 8 * 8
    fold = pltpu.VMEM((count + 3, lon_cells, LANES), F32)
    pairs = pltpu.VMEM((tiles, 8, LANES), F32)
    dma = pltpu.SemaphoreType.DMA
    vmem = pl.BlockSpec(memory_space=pltpu.VMEM)
    values, gains = pl.pallas_call(
        lambda *refs: step(tiles, *refs),
        out_shape=(pltpu.VMEM(operands[0].shape, F32), flat),
        in_specs=[hbm] * 12, out_specs=(vmem, vmem),
        scratch_shapes=[pltpu.VMEM(x.shape, x.dtype) for x in operands] + [
            flat, flat, fold, fold, fold,
            pltpu.VMEM((count + 2, rows, LANES), F32), pltpu.VMEM((count + 2, rows, LANES), F32),
            pltpu.VMEM((count + 1, rows, LANES), F32), pltpu.VMEM((count + 1, rows, LANES), F32),
            pairs, pairs, dma((12,)), dma((3,)), dma((3,)),
            dma((tiles,)), dma((tiles,)), dma],
        compiler_params=pltpu.CompilerParams(
            collective_id=0, has_side_effects=True, vmem_limit_bytes=32 << 20),
        name="ocean_step",
    )(*[pltpu.with_memory_space_constraint(x, pltpu.HBM) for x in operands])
    result = pl.pallas_call(
        lambda *refs: finish(lon_cells, *refs),
        out_shape=pltpu.HBM(values.shape, F32),
        in_specs=[vmem, vmem], out_specs=hbm,
        scratch_shapes=[pltpu.VMEM(values.shape, F32), dma((pl.cdiv(levels, CHUNK),))],
        name="finish",
    )(*[pltpu.with_memory_space_constraint(x, pltpu.VMEM) for x in (values, gains)])
    return result.reshape(count, levels, lon_cells, LANES).transpose(0, 2, 1, 3)


def solution(mesh):
    placed = (
        P(None, "lon", None, "ens"),
        P("lon", None, "ens"),
        P("lon", None, "ens"),
        P("lon", None, "ens"),
        P("lon", None, "ens"),
        P("lon", None, "ens"),
        P("lon", "ens"),
        P("ens", "lon"),
        P(("ens", "lon"), None),
        P(("ens", "lon")),
        P(("ens", "lon")),
        P(("ens", "lon")),
    )
    return jax.shard_map(
        shards, mesh=mesh, in_specs=placed, out_specs=P(None, "lon", None, "ens"), check_vma=False
    )
```

```python
import jax
import jax.numpy as jnp
from jax import lax
from jax.experimental import pallas as pl
from jax.experimental.pallas import tpu as pltpu
from jax.sharding import PartitionSpec as P

CAP = 64
CHUNK = 15
LANES = 128
F32 = jnp.float32
BF16 = jnp.bfloat16
I32 = jnp.int32


def iota(shape, axis):
    return lax.broadcasted_iota(I32, shape, axis)


def thirds(x):
    high = x.astype(BF16).astype(F32)
    rest = x - high
    middle = rest.astype(BF16).astype(F32)
    return high, middle, rest - middle


def route(tiles, tile, source, cells, weight, air, send_ref):
    count, air_cells = air.shape
    records = tile.shape[1]
    picks = (iota((air_cells, records), 0) == source).astype(F32).astype(BF16)
    parts = jnp.concatenate(thirds(air), axis=0).astype(BF16)
    found = jnp.dot(parts, picks, preferred_element_type=F32)
    found = found[:count] + (found[count:2 * count] + found[2 * count:])
    payload = weight * found

    chosen = (iota((tiles, records), 0) == tile).astype(F32)
    earlier = (iota((LANES, LANES), 0) < iota((LANES, LANES), 1)).astype(F32).astype(BF16)
    carried = jnp.zeros((tiles, 1), F32)
    slots = []
    for start in range(0, records, LANES):
        piece = chosen[:, start:start + LANES]
        rank = jnp.dot(piece.astype(BF16), earlier, preferred_element_type=F32) + carried
        slots.append(jnp.sum(piece * rank, axis=0, keepdims=True))
        carried = carried + jnp.sum(piece, axis=1, keepdims=True)
    slot = jnp.concatenate(slots, axis=1)
    places = (iota((CAP, records), 0).astype(F32) == slot).astype(F32).astype(BF16)

    row = (cells >> 7).astype(F32)
    column = (cells & (LANES - 1)).astype(F32)
    lines = [p[n:n + 1] for p in thirds(payload) for n in range(count)] + [row, column]
    spread = jnp.concatenate([(chosen * line).astype(BF16) for line in lines], axis=0)
    packed = lax.dot_general(spread, places, (((1,), (1,)), ((), ())), preferred_element_type=F32)

    def part(index):
        return packed[index * tiles:(index + 1) * tiles]

    send_ref[...] = jnp.zeros(send_ref.shape, F32)
    for n in range(count):
        send_ref[:, n, :CAP] = part(n) + (part(count + n) + part(2 * count + n))
    send_ref[:, count, :CAP] = part(3 * count)
    send_ref[:, count + 1, :CAP] = part(3 * count + 1)


def gathered(received, count, lon_cells):
    surface = jnp.zeros((3 * count * lon_cells, LANES), F32)
    for s in range(received.shape[0]):
        rows = received[s]
        hit = iota((lon_cells, LANES), 0).astype(F32) == rows[count:count + 1]
        lines = [p[n:n + 1] for p in thirds(rows[:count]) for n in range(count)]
        spread = jnp.concatenate(
            [jnp.where(hit, line, 0.0).astype(BF16) for line in lines], axis=0)
        spots = (iota((LANES, LANES), 0).astype(F32) == rows[count + 1:count + 2]).astype(F32)
        surface = surface + lax.dot_general(
            spread, spots.astype(BF16), (((1,), (1,)), ((), ())), preferred_element_type=F32)
    fluxes = []
    for n in range(count):
        block = [surface[(p * count + n) * lon_cells:(p * count + n + 1) * lon_cells]
                 for p in range(3)]
        fluxes.append(block[0] + (block[1] + block[2]))
    return fluxes


def weights(speed, near, far, open_face):
    half = 0.5 * (near + far)
    return (jnp.where(open_face, jnp.maximum(speed, 0.0) + half, 0.0),
            jnp.where(open_face, jnp.minimum(speed, 0.0) - half, 0.0))


def step(tiles, *refs):
    sources, refs = refs[:12], refs[12:]
    values, gains, refs = refs[0], refs[1], refs[2:]
    held, refs = refs[:12], refs[12:]
    (factor, share, top, fold_out, fold_in, right_out, right_in, left_out, left_in,
     send, received, load_sems, out_sems, in_sems, pair_out, pair_in, own_sem) = refs
    (tracer, east, north, kappa, mixing, thickness, depth_ref, air, tile, source, cells,
     weight) = held
    count, planes = tracer.shape[:2]
    lon_cells = depth_ref.shape[0]
    levels = planes // lon_cells
    last = lon_cells - 1

    loads = [pltpu.make_async_copy(a, b, load_sems.at[i])
             for i, (a, b) in enumerate(zip(sources, held))]
    for i in (7, 8, 9, 10, 11, 0, 3, 1, 6, 2, 5, 4):
        loads[i].start()

    me = lax.axis_index("lon")
    right = lax.rem(me + 1, tiles)
    left = lax.rem(me + tiles - 1, tiles)
    partner = tiles - 1 - me
    barrier = pltpu.get_barrier_semaphore()

    @pl.loop(1, tiles)
    def _(hop):
        pl.semaphore_signal(barrier, inc=1, device_id={"lon": lax.rem(me + hop, tiles)},
                            device_id_type=pl.DeviceIdType.MESH)

    for i in (7, 8, 9, 10, 11):
        loads[i].wait()
    route(tiles, tile[...], source[...], cells[...], weight[...], air[...], send)

    for i in (0, 3, 1, 6):
        loads[i].wait()
    depth = depth_ref[...]

    def at(k):
        return pl.ds(pl.multiple_of(k * lon_cells, lon_cells), lon_cells)

    def column(i):
        return pl.ds(i, levels, stride=lon_cells)

    for n in range(count):
        right_out[n, :levels, :] = tracer[n, column(last), :]
        left_out[n, :levels, :] = tracer[n, column(0), :]
    right_out[count, :levels, :] = kappa[column(last), :]
    left_out[count, :levels, :] = kappa[column(0), :]
    right_out[count + 1, :levels, :] = east[column(last), :]
    right_out[count, levels:levels + 1, :] = depth[last:, :].astype(F32)
    left_out[count, levels:levels + 1, :] = depth[:1, :].astype(F32)

    pl.semaphore_wait(barrier, tiles - 1)
    copies = []

    def start(a, b, device):
        index = len(copies)
        copies.append(pltpu.make_async_remote_copy(
            src_ref=a, dst_ref=b, send_sem=out_sems.at[index], recv_sem=in_sems.at[index],
            device_id={"lon": device}, device_id_type=pl.DeviceIdType.MESH))
        copies[-1].start()

    @pl.loop(1, tiles)
    def _(hop):
        other = lax.rem(me + hop, tiles)
        pltpu.make_async_remote_copy(
            src_ref=send.at[other], dst_ref=received.at[me], send_sem=pair_out.at[other],
            recv_sem=pair_in.at[me], device_id={"lon": other},
            device_id_type=pl.DeviceIdType.MESH).start()

    start(right_out, right_in, right)
    start(left_out, left_in, left)


    loads[2].wait()
    lane = iota((lon_cells, LANES), 1)

    def take(k, packed):
        fields = [tracer[n, at(k), :] for n in range(count)] + [kappa[at(k), :], north[at(k), :]]
        return tuple(jnp.where(lane == k, pltpu.roll(x, k + 1, 1), p)
                     for x, p in zip(fields, packed))

    empty = jnp.zeros((lon_cells, LANES), F32)
    packed = lax.fori_loop(0, levels, take, (empty,) * (count + 2), unroll=15)
    packed += (jnp.broadcast_to(depth[:, LANES - 1:].astype(F32), (lon_cells, LANES)),)
    for f, plane in enumerate(packed):
        top[f] = plane
        for i in range(lon_cells):
            fold_out[f, last - i:last - i + 1, :] = plane[i:i + 1]

    start(fold_out, fold_in, partner)
    own = pltpu.make_async_copy(send.at[me], received.at[me], own_sem)
    own.start()
    for i in (5, 4):
        loads[i].wait()

    row = iota((lon_cells, LANES), 0)
    depth_east = jnp.where(row == last, 0, pltpu.roll(depth, last, 0))
    depth_north = jnp.where(lane == LANES - 1, 0, pltpu.roll(depth, LANES - 1, 1))
    open_east = jnp.minimum(depth, depth_east)
    open_north = jnp.minimum(depth, depth_north)

    def inner(k, state):
        prior, gain = state
        here = thickness[at(k), :]
        below = thickness[at(jnp.minimum(k + 1, levels - 1)), :]
        coupling = jnp.where(depth > k + 1, mixing[at(k), :] / (0.5 * (here + below)), 0.0)
        scale = 1.0 / (here + coupling + prior - prior * gain)
        gain = coupling * scale
        gains[at(k), :] = gain
        factor[at(k), :] = prior * scale
        part = here * scale
        share[at(k), :] = part
        spread = kappa[at(k), :]
        ea, eb = weights(east[at(k), :], spread, pltpu.roll(spread, last, 0), open_east > k)
        na, nb = weights(north[at(k), :], spread, pltpu.roll(spread, LANES - 1, 1), open_north > k)
        for n in range(count):
            t = tracer[n, at(k), :]
            zonal = ea * t + eb * pltpu.roll(t, last, 0)
            up = na * t + nb * pltpu.roll(t, LANES - 1, 1)
            stepped = (t - (zonal - pltpu.roll(zonal, 1, 0))) - (up - pltpu.roll(up, 1, 1))
            values[n, at(k), :] = part * stepped
        return coupling, gain

    lax.fori_loop(0, levels, inner, (empty, empty), unroll=3)

    for copy in copies:
        copy.wait()
    deep = iota((levels, LANES), 0)

    first_share = share[column(0), :]
    last_share = share[column(last), :]
    wa, wb = weights(right_in[count + 1, :levels, :], right_in[count, :levels, :],
                     kappa[column(0), :],
                     deep < jnp.minimum(right_in[count, levels:levels + 1, :].astype(I32), depth[:1]))
    ea, eb = weights(east[column(last), :], kappa[column(last), :], left_in[count, :levels, :],
                     deep < jnp.minimum(left_in[count, levels:levels + 1, :].astype(I32), depth[last:]))
    for n in range(count):
        flux = wa * right_in[n, :levels, :] + wb * tracer[n, column(0), :]
        values[n, column(0), :] = values[n, column(0), :] + first_share * flux
        flux = ea * tracer[n, column(last), :] + eb * left_in[n, :levels, :]
        values[n, column(last), :] = values[n, column(last), :] - last_share * flux
    fa, fb = weights(0.5 * (top[count + 1] - fold_in[count + 1]), top[count], fold_in[count],
                     lane < jnp.minimum(top[count + 2], fold_in[count + 2]).astype(I32))
    fold = [fa * top[n] + fb * fold_in[n] for n in range(count)]

    own.wait()

    @pl.loop(1, tiles)
    def _(hop):
        other = lax.rem(me + hop, tiles)
        pltpu.make_async_remote_copy(
            src_ref=send.at[other], dst_ref=received.at[other], send_sem=pair_out.at[other],
            recv_sem=pair_in.at[other], device_id={"lon": other},
            device_id_type=pl.DeviceIdType.MESH).wait()

    surface = gathered(received, count, lon_cells)
    pivot = share[at(0), :] / thickness[at(0), :]
    for n in range(count):
        values[n, at(0), :] = values[n, at(0), :] + jnp.where(depth > 0, surface[n] * pivot, 0.0)

    def down(k, value):
        part = jnp.where(lane == LANES - 1, share[at(k), :], 0.0)
        mult = factor[at(k), :]
        solved = []
        for n in range(count):
            own_part = values[n, at(k), :] - part * pltpu.roll(fold[n], LANES - 1 - k, 1)
            solved.append(own_part + mult * value[n])
            values[n, at(k), :] = solved[n]
        return tuple(solved)

    value = lax.fori_loop(0, levels, down, (empty,) * count, unroll=15)


def finish(lon_cells, values, gains, out, solved, sems):
    count, planes = values.shape[:2]
    levels = planes // lon_cells

    def at(k):
        return pl.ds(pl.multiple_of(k * lon_cells, lon_cells), lon_cells)

    stores = []
    value = (jnp.zeros((lon_cells, LANES), F32),) * count
    for index, end in enumerate(range(levels, 0, -CHUNK)):
        begin = max(end - CHUNK, 0)

        def up(move, value, end=end):
            k = end - 1 - move
            gain = gains[at(k), :]
            value = tuple(values[n, at(k), :] + gain * value[n] for n in range(count))
            for n in range(count):
                solved[n, at(k), :] = value[n]
            return value

        value = lax.fori_loop(0, end - begin, up, value, unroll=CHUNK)
        block = pl.ds(begin * lon_cells, (end - begin) * lon_cells)
        stores.append(pltpu.make_async_copy(
            solved.at[:, block], out.at[:, block], sems.at[index]))
        stores[-1].start()
    for store in stores:
        store.wait()


def shards(tracer, east_speed, north_speed, diffusivity, mixing, thickness, depth_levels,
           air_flux, margin_tile, margin_source, margin_cell, margin_weight):
    count, lon_cells, levels, lat_cells = tracer.shape
    tiles = lax.axis_size("lon")
    records = margin_source.shape[0]
    assert lat_cells == LANES and levels < LANES

    def by_level(x):
        return x.transpose(1, 0, 2).reshape(levels * lon_cells, LANES)

    operands = (
        tracer.transpose(0, 2, 1, 3).reshape(count, levels * lon_cells, LANES),
        *[by_level(x) for x in (east_speed, north_speed, diffusivity, mixing, thickness)],
        depth_levels, air_flux,
        *[x.reshape(1, records) for x in (margin_tile, margin_source, margin_cell, margin_weight)])
    hbm = pl.BlockSpec(memory_space=pltpu.HBM)
    flat = pltpu.VMEM((levels * lon_cells, LANES), F32)
    rows = (levels + 8) // 8 * 8
    fold = pltpu.VMEM((count + 3, lon_cells, LANES), F32)
    pairs = pltpu.VMEM((tiles, 8, LANES), F32)
    dma = pltpu.SemaphoreType.DMA
    vmem = pl.BlockSpec(memory_space=pltpu.VMEM)
    values, gains = pl.pallas_call(
        lambda *refs: step(tiles, *refs),
        out_shape=(pltpu.VMEM(operands[0].shape, F32), flat),
        in_specs=[hbm] * 12, out_specs=(vmem, vmem),
        scratch_shapes=[pltpu.VMEM(x.shape, x.dtype) for x in operands] + [
            flat, flat, fold, fold, fold,
            pltpu.VMEM((count + 2, rows, LANES), F32), pltpu.VMEM((count + 2, rows, LANES), F32),
            pltpu.VMEM((count + 1, rows, LANES), F32), pltpu.VMEM((count + 1, rows, LANES), F32),
            pairs, pairs, dma((12,)), dma((3,)), dma((3,)),
            dma((tiles,)), dma((tiles,)), dma],
        compiler_params=pltpu.CompilerParams(
            collective_id=0, has_side_effects=True, vmem_limit_bytes=32 << 20),
        name="ocean_step",
    )(*[pltpu.with_memory_space_constraint(x, pltpu.HBM) for x in operands])
    result = pl.pallas_call(
        lambda *refs: finish(lon_cells, *refs),
        out_shape=pltpu.HBM(values.shape, F32),
        in_specs=[vmem, vmem], out_specs=hbm,
        scratch_shapes=[pltpu.VMEM(values.shape, F32), dma((pl.cdiv(levels, CHUNK),))],
        name="finish",
    )(*[pltpu.with_memory_space_constraint(x, pltpu.VMEM) for x in (values, gains)])
    return result.reshape(count, levels, lon_cells, LANES).transpose(0, 2, 1, 3)


def solution(mesh):
    placed = (
        P(None, "lon", None, "ens"),
        P("lon", None, "ens"),
        P("lon", None, "ens"),
        P("lon", None, "ens"),
        P("lon", None, "ens"),
        P("lon", None, "ens"),
        P("lon", "ens"),
        P("ens", "lon"),
        P(("ens", "lon"), None),
        P(("ens", "lon")),
        P(("ens", "lon")),
        P(("ens", "lon")),
    )
    return jax.shard_map(
        shards, mesh=mesh, in_specs=placed, out_specs=P(None, "lon", None, "ens"), check_vma=False
    )
```
